32 devices in a mesh: rep: 4 (over x, core), fsdp: 2 (over y), cp: 4 (over z).
Axes of the slice: x: 2, y: 2, z: 4, core: 2. Of those that a mesh axis runs over, the one named last changes fastest.
Arguments:
- tokens: bfloat16 [8, 512, 1024], P(('rep', 'fsdp'), 'cp'), may hold values from -6 to 6
- segments: int32 [8, 512], P(('rep', 'fsdp'), 'cp'), may hold values from 0 to 15, never falling along the last dimension, each value on 1 to 64 neighbouring positions
- cotangent: bfloat16 [8, 512, 1024], P(('rep', 'fsdp'), 'cp'), may hold values from -6 to 6
- w_qkv: bfloat16 [1024, 3072], P(('fsdp', 'cp')), may hold values from -8 to 8
- w_attn: bfloat16 [1024, 1024], P(('fsdp', 'cp')), may hold values from -0.75 to 0.75
- w_in: bfloat16 [1024, 5248], P(('fsdp', 'cp')), may hold values from -0.1875 to 0.1875
- w_mlp: bfloat16 [2624, 1024], P(None, ('fsdp', 'cp')), may hold values from -0.125 to 0.125
- gain_attn: bfloat16 [1024], P(('fsdp', 'cp')), may hold values from 0.3984375 to 1.59375
- gain_mlp: bfloat16 [1024], P(('fsdp', 'cp')), may hold values from 0.3984375 to 1.59375
Outputs:
- output: bfloat16 [8, 512, 1024], P(('rep', 'fsdp'), 'cp')
- grad_tokens: bfloat16 [8, 512, 1024], P(('rep', 'fsdp'), 'cp')
- grad_qkv: float32 [1024, 3072], P(('fsdp', 'cp'))
- grad_attn: float32 [1024, 1024], P(('fsdp', 'cp'))
- grad_in: float32 [1024, 5248], P(('fsdp', 'cp'))
- grad_mlp: float32 [2624, 1024], P(None, ('fsdp', 'cp'))
- grad_gain_attn: float32 [1024], P(('fsdp', 'cp'))
- grad_gain_mlp: float32 [1024], P(('fsdp', 'cp'))
The draws below stay inside these ranges and needn't reach their ends.
Inputs may be any that keep to these rules, and one draw needn't show every extreme that they name: `segments`: along each sequence segment ids never fall; each document holds 1 to 64 tokens, and one holds exactly 64.
All inputs are finite; a program needn't handle non-finite values.
Results may differ from the reference program's by a relative error of at most 0.012.
Values may be sent and summed in bfloat16 or wider, within the bound.
A program may use at most 192 MiB of HBM per device.

```python
import math
import jax
import jax.numpy as jnp
import numpy as np
from jax import lax

D = 1024
HEADS = 16
FF = 2624
SEQ_LEN = 512
SEQS = 8
DOC_MOST = 64
DOCS = 16


def draw_w_qkv(key, part):
    base = jnp.clip(jax.random.normal(key, (D, 3 * D), jnp.float32), -6.0, 6.0) * D ** (-0.5)
    return base.astype(jnp.bfloat16)


def spiked(result, own_key, source, target, shards_of, factor):
    def block_of(dim):
        return (jnp.arange(result.shape[dim]) // (result.shape[dim] // shards_of)).reshape((-1,) + (1,) * (result.ndim - 1 - dim))

    first = jax.random.permutation(own_key, shards_of)[block_of(target)]
    other_side = (block_of(target) + shards_of // 2) % shards_of
    return jnp.where((block_of(source) == first) | (block_of(source) == other_side), factor * result, result)


def levels(own_key, dims, pieces, least, high):
    def one(axis_at, shards_of):
        draws = jax.random.uniform(jax.random.fold_in(jax.random.fold_in(own_key, 6), axis_at), (shards_of,), jnp.float32, least / len(pieces), high / len(pieces))
        return jnp.repeat(jnp.exp(draws), dims[axis_at] // shards_of).reshape((-1,) + (1,) * (len(dims) - axis_at - 1))

    factor_of = one(*pieces[0])
    for cut in pieces[1:]:
        factor_of = factor_of * one(*cut)
    return factor_of


def length_profile(number_of, total, reach, skew):
    loads = [(1 << 20) // math.isqrt(standing ** skew) + 1 for standing in range(2, number_of + 1)]
    surplus, holding = total - reach - (number_of - 1), [1] * (number_of - 1)
    while surplus > 0:
        candidates = [i for i in range(number_of - 1) if holding[i] < reach]
        mass, budget = sum([loads[i] for i in candidates]), surplus
        for i in candidates:
            more = min(reach - holding[i], max(1, budget * loads[i] // mass), surplus)
            holding[i] = holding[i] + more
            surplus = surplus - more
    return np.array([reach] + holding)


def ragged(key, amount, total, limit, skew):
    if amount == 2:
        one = jax.random.randint(key, (), max(1, total - limit), min(limit, total - 1) + 1)
        return jnp.stack([one, total - one])
    lengths = jnp.asarray(length_profile(amount, total, limit, skew), jnp.int32)
    couples = (amount - 1) // 2
    giver, receiver = lengths[1:1 + 2 * couples:2], lengths[2:2 + 2 * couples:2]
    slack = jnp.minimum(giver - 1, limit - receiver)
    moved = jax.random.randint(jax.random.fold_in(key, 1), (couples,), 0, 1 << 20) % (slack + 1)
    lengths = lengths.at[1:1 + 2 * couples:2].set(giver - moved).at[2:2 + 2 * couples:2].set(receiver + moved)
    return lengths[jax.random.permutation(jax.random.fold_in(key, 2), amount)]


def scatter_about(key, extent, spread, bound, pieces=(), held_as=jnp.bfloat16):
    loudness = levels(key, extent, pieces, -0.22, 0.18) if pieces else 1.0
    drawn = jax.random.normal(key, extent, jnp.float32) * spread * loudness
    return jnp.minimum(jnp.maximum(drawn, -bound), bound).astype(held_as)


def gaussian_with(stream_key, extent, scale, most, split, heavy, kind=jnp.bfloat16):
    values = scale * jax.random.normal(stream_key, extent, jnp.float32)
    if split:
        values = values * levels(stream_key, extent, split, -0.22, 0.18)
    return jnp.clip(spiked(values, jax.random.fold_in(stream_key, 3), *heavy), -most, most).astype(kind)


def setup_inputs(seed: int = 0) -> dict:
    arg_keys = jax.random.split(jax.random.key(seed), 10)
    tokens = scatter_about(arg_keys[0], (SEQS, SEQ_LEN, D), 1.0, 6.0, ((0, 8), (1, 4)))
    segments = jax.vmap(lambda own: jnp.searchsorted(jnp.cumsum(ragged(own, DOCS, SEQ_LEN, DOC_MOST, 1)), jnp.arange(SEQ_LEN), side="right"))(jax.random.split(arg_keys[1], SEQS)).reshape((SEQS, SEQ_LEN)).astype(jnp.int32)
    cotangent = gaussian_with(arg_keys[2], (SEQS, SEQ_LEN, D), 1.0, 6.0, ((0, 8), (1, 4)), (1, 2, 4, 2.0))
    w_qkv = draw_w_qkv(jax.random.fold_in(arg_keys[9], 71), 0)
    w_attn = scatter_about(arg_keys[4], (D, D), (D // 16) ** -0.5, 0.75, ((0, 8),))
    w_in = scatter_about(arg_keys[5], (D, 2 * FF), D ** -0.5, 0.1875, ((0, 8),))
    w_mlp = scatter_about(arg_keys[6], (FF, D), FF ** -0.5, 0.125, ((1, 8),))
    gain_attn = jnp.clip(1.0 + 0.12 * jax.random.normal(arg_keys[7], (D,), jnp.float32), 0.3984375, 1.59375).astype(jnp.bfloat16)
    gain_mlp = jnp.clip(1.0 + 0.12 * jax.random.normal(arg_keys[8], (D,), jnp.float32), 0.3984375, 1.59375).astype(jnp.bfloat16)
    return dict(tokens=tokens, segments=segments, cotangent=cotangent, w_qkv=w_qkv, w_attn=w_attn, w_in=w_in, w_mlp=w_mlp, gain_attn=gain_attn, gain_mlp=gain_mlp)


EPS = 1e-05
THETA = 160000.0
NEG = -1e+30
GROUP = 4

def layer_norm(values):
    mean = lax.optimization_barrier(jnp.mean(values, -1, keepdims=True))
    centred = values - mean
    var = lax.optimization_barrier(jnp.mean(centred * centred, -1, keepdims=True))
    rstd = lax.rsqrt(var + EPS)
    return (centred * rstd, rstd)

def norm_back(grad_norm, normed, rstd):
    mean_grad = lax.optimization_barrier(jnp.mean(grad_norm, -1, keepdims=True))
    mean_dot = lax.optimization_barrier(jnp.mean(grad_norm * normed, -1, keepdims=True))
    return (grad_norm - mean_grad - normed * mean_dot) * rstd

def rope_tables(positions, half):
    index = jnp.arange(half, dtype=jnp.float32)
    inverse = jnp.exp(-(2.0 * index / (2.0 * half)) * math.log(THETA))
    angle = positions[:, None] * inverse[None, :]
    return (jnp.cos(angle)[:, None, :], jnp.sin(angle)[:, None, :])

def rotate(values, cosine, sine):
    half = cosine.shape[-1]
    first, second = (values[..., :half], values[..., half:])
    return jnp.concatenate([first * cosine - second * sine, second * cosine + first * sine], -1)

def unrotate(values, cosine, sine):
    half = cosine.shape[-1]
    first, second = (values[..., :half], values[..., half:])
    return jnp.concatenate([first * cosine + second * sine, second * cosine - first * sine], -1)

def gelu_parts(values):
    cdf = 0.5 * (1.0 + jax.scipy.special.erf(values / math.sqrt(2.0)))
    slope = cdf + values * jnp.exp(-0.5 * values * values) / math.sqrt(2.0 * math.pi)
    return (values * cdf, slope)

def split_groups(values):
    rows, heads, width = values.shape
    return values.reshape(rows, heads // GROUP, GROUP, width).transpose(1, 0, 2, 3)

def join_groups(values):
    groups, rows, heads, width = values.shape
    return values.transpose(1, 0, 2, 3).reshape(rows, groups * heads, width)

def scores(query, keys, same):
    scale = 1.0 / math.sqrt(query.shape[-1])
    raw = jnp.einsum('nhe,lhe->hnl', query.astype(jnp.float32), keys.astype(jnp.float32)) * scale
    return jnp.where(same[None], raw, NEG)

def attend(query, keys, values, same):

    def one(group):
        qg, kg, vg = group
        logits = scores(qg, kg, same)
        top = lax.optimization_barrier(jnp.max(logits, -1, keepdims=True))
        lse = top + jnp.log(lax.optimization_barrier(jnp.sum(jnp.exp(logits - top), -1, keepdims=True)))
        probs = jnp.exp(logits - lse).astype(jnp.bfloat16)
        mixed = jnp.einsum('hnl,lhe->nhe', probs.astype(jnp.float32), vg.astype(jnp.float32))
        return (mixed, lse)
    mixed, lse = lax.map(one, (split_groups(query), split_groups(keys), split_groups(values)))
    return (join_groups(mixed), lse)

def attend_back(query, keys, values, mixed, grad_mixed, lse, same):
    scale = 1.0 / math.sqrt(query.shape[-1])

    def one(group):
        qg, kg, vg, og, dog, lg = group
        logits = scores(qg, kg, same)
        probs = jnp.exp(logits - lg)
        probs_b = probs.astype(jnp.bfloat16)
        dog_f = dog.astype(jnp.float32)
        grad_v = jnp.einsum('hnl,nhe->lhe', probs_b.astype(jnp.float32), dog_f)
        grad_p = jnp.einsum('nhe,lhe->hnl', dog_f, vg.astype(jnp.float32))
        delta = lax.optimization_barrier(jnp.sum(dog_f * og.astype(jnp.float32), -1)).transpose(1, 0)
        grad_s = (probs * (grad_p - delta[..., None])).astype(jnp.bfloat16).astype(jnp.float32)
        grad_q = jnp.einsum('hnl,lhe->nhe', grad_s, kg.astype(jnp.float32)) * scale
        grad_k = jnp.einsum('hnl,nhe->lhe', grad_s, qg.astype(jnp.float32)) * scale
        return (grad_q, grad_k, grad_v)
    parts = (split_groups(query), split_groups(keys), split_groups(values), split_groups(mixed), split_groups(grad_mixed), lse)
    grad_q, grad_k, grad_v = lax.map(one, parts)
    return (join_groups(grad_q), join_groups(grad_k), join_groups(grad_v))

def one_sequence(tokens, segments, cotangent, weights):
    w_qkv, w_attn, w_in, w_mlp, gain_attn, gain_mlp = weights
    length = tokens.shape[0]
    width = tokens.shape[1]
    hidden = w_mlp.shape[0]
    heads = HEADS
    size = width // heads
    g_one = gain_attn.astype(jnp.float32)
    g_two = gain_mlp.astype(jnp.float32)
    index = jnp.arange(length, dtype=jnp.int32)
    start = lax.optimization_barrier(jnp.sum((segments[None, :] < segments[:, None]).astype(jnp.int32), 1))
    cosine, sine = rope_tables((index - start).astype(jnp.float32), size // 2)
    same = segments[:, None] == segments[None, :]
    inputs = tokens.astype(jnp.float32)
    n_one, r_one = layer_norm(inputs)
    h_one = (n_one * g_one).astype(jnp.bfloat16)
    qkv = jnp.dot(h_one, w_qkv, preferred_element_type=jnp.float32).reshape(length, 3, heads, size)
    query = rotate(qkv[:, 0], cosine, sine).astype(jnp.bfloat16)
    keys = rotate(qkv[:, 1], cosine, sine).astype(jnp.bfloat16)
    values = qkv[:, 2].astype(jnp.bfloat16)
    mixed, lse = attend(query, keys, values, same)
    mixed_b = mixed.astype(jnp.bfloat16)
    flat_mixed = mixed_b.reshape(length, width)
    x_two = inputs + jnp.dot(flat_mixed, w_attn, preferred_element_type=jnp.float32)
    n_two, r_two = layer_norm(x_two)
    h_two = (n_two * g_two).astype(jnp.bfloat16)
    proj = jnp.dot(h_two, w_in, preferred_element_type=jnp.float32)
    act_in, gate = (proj[:, :hidden], proj[:, hidden:])
    act, slope = gelu_parts(act_in)
    inner = (act * gate).astype(jnp.bfloat16)
    output = (x_two + jnp.dot(inner, w_mlp, preferred_element_type=jnp.float32)).astype(jnp.bfloat16)
    grad_out = cotangent.astype(jnp.float32)
    grad_mlp = jnp.dot(inner.T, cotangent, preferred_element_type=jnp.float32)
    grad_inner = jnp.dot(cotangent, w_mlp.T, preferred_element_type=jnp.float32)
    grad_proj = jnp.concatenate([grad_inner * gate * slope, grad_inner * act], -1).astype(jnp.bfloat16)
    grad_in = jnp.dot(h_two.T, grad_proj, preferred_element_type=jnp.float32)
    grad_h_two = jnp.dot(grad_proj, w_in.T, preferred_element_type=jnp.float32)
    grad_g_two = lax.optimization_barrier(jnp.sum(grad_h_two * n_two, 0))
    grad_x_two = grad_out + norm_back(grad_h_two * g_two, n_two, r_two)
    grad_a = grad_x_two.astype(jnp.bfloat16)
    grad_attn = jnp.dot(flat_mixed.T, grad_a, preferred_element_type=jnp.float32)
    grad_mixed = jnp.dot(grad_a, w_attn.T, preferred_element_type=jnp.float32).astype(jnp.bfloat16)
    grad_q, grad_k, grad_v = attend_back(query, keys, values, mixed_b, grad_mixed.reshape(length, heads, size), lse, same)
    grad_q = unrotate(grad_q, cosine, sine)
    grad_k = unrotate(grad_k, cosine, sine)
    grad_qkv_rows = jnp.stack([grad_q, grad_k, grad_v], 1).reshape(length, 3 * width).astype(jnp.bfloat16)
    grad_qkv = jnp.dot(h_one.T, grad_qkv_rows, preferred_element_type=jnp.float32)
    grad_h_one = jnp.dot(grad_qkv_rows, w_qkv.T, preferred_element_type=jnp.float32)
    grad_g_one = lax.optimization_barrier(jnp.sum(grad_h_one * n_one, 0))
    grad_tokens = (grad_x_two + norm_back(grad_h_one * g_one, n_one, r_one)).astype(jnp.bfloat16)
    return (output, grad_tokens, (grad_qkv, grad_attn, grad_in, grad_mlp, grad_g_one, grad_g_two))

def reference(tokens, segments, cotangent, w_qkv, w_attn, w_in, w_mlp, gain_attn, gain_mlp):
    weights = (w_qkv, w_attn, w_in, w_mlp, gain_attn, gain_mlp)
    zeros = tuple((jnp.zeros(w.shape, jnp.float32) for w in weights))

    def step(totals, item):
        seq_tokens, seq_segments, seq_cotangent = item
        output, grad_tokens, grads = one_sequence(seq_tokens, seq_segments, seq_cotangent, weights)
        totals = tuple((a + b for a, b in zip(totals, grads)))
        return (totals, (output, grad_tokens))
    totals, (output, grad_tokens) = lax.scan(step, zeros, (tokens, segments, cotangent))
    return (output, grad_tokens, totals[0], totals[1], totals[2], totals[3], totals[4], totals[5])
```

```python
import math

import jax
import jax.numpy as jnp
from jax import lax
from jax.sharding import PartitionSpec as P

HEADS = 16


EPS = 1e-05
THETA = 160000.0
NEG = -1e30
GROUP = 4


def from_behind(value, axis, steps):
    count = lax.axis_size(axis)
    initial, last = (max(0, -steps), min(count, count - steps))
    return lax.ppermute(value, axis, [(source, source + steps) for source in range(initial, last)])


def layer_norm(values):
    mean = jnp.mean(values, -1, keepdims=True)
    centred = values - mean
    var = jnp.mean(centred * centred, -1, keepdims=True)
    rstd = lax.rsqrt(var + EPS)
    return (centred * rstd, rstd)


def norm_back(grad_norm, normed, rstd):
    mean_grad = jnp.mean(grad_norm, -1, keepdims=True)
    mean_dot = jnp.mean(grad_norm * normed, -1, keepdims=True)
    return (grad_norm - mean_grad - normed * mean_dot) * rstd


def rope_tables(positions, half):
    index = jnp.arange(half, dtype=jnp.float32)
    inverse = jnp.exp(-(2.0 * index / (2.0 * half)) * math.log(THETA))
    angle = positions[:, None] * inverse[None, :]
    return (jnp.cos(angle)[:, None, :], jnp.sin(angle)[:, None, :])


def rotate(values, cosine, sine):
    half = cosine.shape[-1]
    first, second = (values[..., :half], values[..., half:])
    return jnp.concatenate([first * cosine - second * sine, second * cosine + first * sine], -1)


def unrotate(values, cosine, sine):
    half = cosine.shape[-1]
    first, second = (values[..., :half], values[..., half:])
    return jnp.concatenate([first * cosine + second * sine, second * cosine - first * sine], -1)


def gelu_parts(values):
    cdf = 0.5 * (1.0 + jax.scipy.special.erf(values / math.sqrt(2.0)))
    slope = cdf + values * jnp.exp(-0.5 * values * values) / math.sqrt(2.0 * math.pi)
    return (values * cdf, slope)


def split_groups(values):
    rows, heads, width = values.shape
    return values.reshape(rows, heads // GROUP, GROUP, width).transpose(1, 0, 2, 3)


def join_groups(values):
    groups, rows, heads, width = values.shape
    return values.transpose(1, 0, 2, 3).reshape(rows, groups * heads, width)


def scores(query, keys, same):
    scale = 1.0 / math.sqrt(query.shape[-1])
    raw = jnp.einsum("nhe,lhe->hnl", query, keys, preferred_element_type=jnp.float32) * scale
    return jnp.where(same[None], raw, NEG)


def attend(query, keys, values, same):

    def one(group):
        qg, kg, vg = group
        logits = scores(qg, kg, same)
        top = jnp.max(logits, -1, keepdims=True)
        lse = top + jnp.log(jnp.sum(jnp.exp(logits - top), -1, keepdims=True))
        probs = jnp.exp(logits - lse).astype(jnp.bfloat16)
        mixed = jnp.einsum("hnl,lhe->nhe", probs, vg, preferred_element_type=jnp.float32)
        return (mixed, lse)

    mixed, lse = lax.map(one, (split_groups(query), split_groups(keys), split_groups(values)))
    return (join_groups(mixed), lse)


def attend_back(query, keys, values, mixed, grad_mixed, lse, same):
    scale = 1.0 / math.sqrt(query.shape[-1])

    def one(group):
        qg, kg, vg, og, dog, lg = group
        logits = scores(qg, kg, same)
        probs = jnp.exp(logits - lg)
        probs_b = probs.astype(jnp.bfloat16)
        grad_v = jnp.einsum("hnl,nhe->lhe", probs_b, dog, preferred_element_type=jnp.float32)
        grad_p = jnp.einsum("nhe,lhe->hnl", dog, vg, preferred_element_type=jnp.float32)
        delta = jnp.sum(dog.astype(jnp.float32) * og.astype(jnp.float32), -1).transpose(1, 0)
        grad_s = (probs * (grad_p - delta[..., None])).astype(jnp.bfloat16)
        grad_q = jnp.einsum("hnl,lhe->nhe", grad_s, kg, preferred_element_type=jnp.float32) * scale
        grad_k = jnp.einsum("hnl,nhe->lhe", grad_s, qg, preferred_element_type=jnp.float32) * scale
        return (grad_q, grad_k, grad_v)

    parts = (
        split_groups(query),
        split_groups(keys),
        split_groups(values),
        split_groups(mixed),
        split_groups(grad_mixed),
        lse,
    )
    grad_q, grad_k, grad_v = lax.map(one, parts)
    return (join_groups(grad_q), join_groups(grad_k), join_groups(grad_v))


def fetch_near(keys_local, values_local, reach):
    width = keys_local.shape[1]
    both = jnp.concatenate([keys_local, values_local], 1)
    parts = []
    for offset in range(-reach, reach + 1):
        parts.append(both if offset == 0 else from_behind(both, "cp", -offset))
    joined = jnp.concatenate(parts, 0)
    return (joined[:, :width], joined[:, width:])


def return_near(grad_keys, grad_values, reach, rows):
    width = grad_keys.shape[1]
    own_k = grad_keys[reach * rows : (reach + 1) * rows]
    own_v = grad_values[reach * rows : (reach + 1) * rows]
    both = jnp.concatenate([grad_keys, grad_values], 1).astype(jnp.bfloat16)
    for offset in range(-reach, reach + 1):
        if offset != 0:
            lower = (reach + offset) * rows
            got = from_behind(both[lower : lower + rows], "cp", offset).astype(jnp.float32)
            own_k = own_k + got[:, :width]
            own_v = own_v + got[:, width:]
    return (own_k, own_v)


def swap(value, axis, mask):
    return lax.ppermute(value, axis, [(i, i ^ mask) for i in range(lax.axis_size(axis))])


def side(axis, mask):
    return (lax.axis_index(axis) // mask) % 2


def masks(axis):
    found = []
    mask = lax.axis_size(axis) // 2
    while mask:
        found.append((axis, mask))
        mask //= 2
    return found


def digits():
    return masks("fsdp") + masks("cp") + masks("rep")


def order(turn):
    rep = masks("rep")
    rest = [rep[:-1], masks("fsdp"), masks("cp")[::-1]]
    steps = rep[-1:]
    for i in range(3):
        steps = steps + rest[(turn + i) % 3]
    return steps


def reduce_rows(value, turn):
    left = digits()
    rows, columns = value.shape
    value = value.reshape([2] * len(left) + [rows // 2 ** len(left), columns])
    for axis, mask in order(turn):
        dim = left.index((axis, mask))
        left.remove((axis, mask))
        mine = side(axis, mask)
        keep = lax.dynamic_index_in_dim(value, mine, dim, False).astype(jnp.float32)
        send = lax.dynamic_index_in_dim(value, 1 - mine, dim, False).astype(jnp.bfloat16)
        value = keep + swap(send, axis, mask).astype(jnp.float32)
        if left:
            value = value.astype(jnp.bfloat16)
    for axis, mask in masks("rep"):
        value = value.astype(jnp.bfloat16)
        value = double(value[None] if value.ndim == 2 else value, axis, mask)
    if masks("rep"):
        count = len(masks("rep"))
        value = value.reshape([2] * count + list(value.shape[-2:]))
        value = value.transpose(list(range(count))[::-1] + [count, count + 1])
    return value.reshape(-1, columns).astype(jnp.float32)


def double(value, axis, mask):
    mine = side(axis, mask)
    got = swap(value, axis, mask)
    return jnp.stack([jnp.where(mine == 0, value, got), jnp.where(mine == 0, got, value)])


def gather_rows(local, turn):
    copies = lax.axis_size("rep")
    rows, columns = local.shape
    part = rows // copies
    value = lax.dynamic_slice_in_dim(local, lax.axis_index("rep") * part, part, 0)
    steps = order(turn)[::-1]
    for axis, mask in steps:
        value = double(value, axis, mask)
    outer = steps[::-1]
    count = len(outer)
    value = value.reshape([2] * count + [part, columns])
    where = [outer.index(digit) for digit in digits()]
    return value.transpose(where + [count, count + 1]).reshape(-1, columns)


def shards(tokens, segments, cotangent, w_qkv, w_attn, w_in, w_mlp, gain_attn, gain_mlp):
    local_tokens = tokens[0]
    local_segments = segments[0]
    local_cotangent = cotangent[0]
    rows, width = local_tokens.shape
    heads = HEADS
    size = width // heads
    blocks = lax.axis_size("cp")
    position = lax.axis_index("cp")
    hidden = w_mlp.shape[0]
    gains = jnp.stack([gain_attn, gain_mlp], 1)
    gains = jnp.pad(gains, ((0, 0), (0, 126)))
    wq = gather_rows(jnp.concatenate([w_qkv[:, :width], gains], 1), 0)
    wk = gather_rows(w_qkv[:, width : 2 * width], 1)
    wv = gather_rows(w_qkv[:, 2 * width :], 2)
    wq, wk, wv, late_attn, late_in, late_mlp = lax.optimization_barrier(
        (wq, wk, wv, w_attn, w_in, w_mlp)
    )
    f_gains = wq[:, width : width + 2].T
    f_gone, f_gtwo = f_gains[0], f_gains[1]
    wq = wq[:, :width]
    f_attn = gather_rows(late_attn, 1)
    wa = gather_rows(late_in[:, :hidden], 0)
    wg = gather_rows(late_in[:, hidden:], 1)
    wm = gather_rows(late_mlp.T, 2)
    key_segments = lax.all_gather(local_segments, "cp", axis=0, tiled=True)
    index = position * rows + jnp.arange(rows, dtype=jnp.int32)
    start = jnp.sum((key_segments[None, :] < local_segments[:, None]).astype(jnp.int32), 1)
    cosine, sine = rope_tables((index - start).astype(jnp.float32), size // 2)
    doc_most = rows * blocks // 8
    reach = min(blocks - 1, (doc_most - 1) // rows + 1)
    g_one = f_gone.astype(jnp.float32)
    g_two = f_gtwo.astype(jnp.float32)
    inputs = local_tokens.astype(jnp.float32)
    n_one, r_one = layer_norm(inputs)
    h_one = (n_one * g_one).astype(jnp.bfloat16)
    key_raw = jnp.dot(h_one, wk, preferred_element_type=jnp.float32).reshape(rows, heads, size)
    keys_local = rotate(key_raw, cosine, sine).astype(jnp.bfloat16).reshape(rows, width)
    values_local = jnp.dot(h_one, wv, preferred_element_type=jnp.float32).astype(jnp.bfloat16)
    query_raw = jnp.dot(h_one, wq, preferred_element_type=jnp.float32).reshape(rows, heads, size)
    query = rotate(query_raw, cosine, sine).astype(jnp.bfloat16)
    offsets = jnp.arange(-reach, reach + 1, dtype=jnp.int32)
    block_ids = position + offsets
    inside = (block_ids >= 0) & (block_ids < blocks)
    clamped = jnp.clip(block_ids, 0, blocks - 1)
    window_segments = jnp.take(key_segments.reshape(blocks, rows), clamped, axis=0).reshape(-1)
    window_inside = jnp.repeat(inside, rows)
    same = (local_segments[:, None] == window_segments[None, :]) & window_inside[None, :]
    keys_flat, values_flat = fetch_near(keys_local, values_local, reach)
    span = keys_flat.shape[0]
    keys = keys_flat.reshape(span, heads, size)
    values = values_flat.reshape(span, heads, size)
    mixed, lse = attend(query, keys, values, same)
    mixed_b = mixed.astype(jnp.bfloat16)
    flat_mixed = mixed_b.reshape(rows, width)
    x_two = inputs + jnp.dot(flat_mixed, f_attn, preferred_element_type=jnp.float32)
    n_two, r_two = layer_norm(x_two)
    h_two = (n_two * g_two).astype(jnp.bfloat16)
    act_in = jnp.dot(h_two, wa, preferred_element_type=jnp.float32)
    gate = jnp.dot(h_two, wg, preferred_element_type=jnp.float32)
    act, slope = gelu_parts(act_in)
    inner = (act * gate).astype(jnp.bfloat16)
    output = (x_two + jnp.dot(inner, wm.T, preferred_element_type=jnp.float32)).astype(
        jnp.bfloat16
    )
    grad_out = local_cotangent.astype(jnp.float32)
    grad_mlp = jnp.dot(local_cotangent.T, inner, preferred_element_type=jnp.float32)
    sum_mlp = reduce_rows(grad_mlp.astype(jnp.bfloat16), 2)
    grad_inner = jnp.dot(local_cotangent, wm, preferred_element_type=jnp.float32)
    grad_act = (grad_inner * gate * slope).astype(jnp.bfloat16)
    grad_gate = (grad_inner * act).astype(jnp.bfloat16)
    grad_ina = jnp.dot(h_two.T, grad_act, preferred_element_type=jnp.float32)
    grad_ing = jnp.dot(h_two.T, grad_gate, preferred_element_type=jnp.float32)
    sum_ina = reduce_rows(grad_ina.astype(jnp.bfloat16), 0)
    sum_ing = reduce_rows(grad_ing.astype(jnp.bfloat16), 1)
    grad_h_two = jnp.dot(grad_act, wa.T, preferred_element_type=jnp.float32) + jnp.dot(
        grad_gate, wg.T, preferred_element_type=jnp.float32
    )
    grad_g_two = jnp.sum(grad_h_two * n_two, 0)
    grad_x_two = grad_out + norm_back(grad_h_two * g_two, n_two, r_two)
    grad_a = grad_x_two.astype(jnp.bfloat16)
    grad_attn = jnp.dot(flat_mixed.T, grad_a, preferred_element_type=jnp.float32)
    sum_attn = reduce_rows(grad_attn.astype(jnp.bfloat16), 1)
    grad_mixed = jnp.dot(grad_a, f_attn.T, preferred_element_type=jnp.float32).astype(jnp.bfloat16)
    back_keys, back_values = (keys, values)
    grad_q, grad_k_all, grad_v_all = attend_back(
        query, back_keys, back_values, mixed_b, grad_mixed.reshape(rows, heads, size), lse, same
    )
    grad_k_own, grad_v_own = return_near(
        grad_k_all.reshape(span, width), grad_v_all.reshape(span, width), reach, rows
    )
    grad_q = unrotate(grad_q, cosine, sine)
    grad_k = unrotate(grad_k_own.reshape(rows, heads, size), cosine, sine)
    row_q = grad_q.reshape(rows, width).astype(jnp.bfloat16)
    row_k = grad_k.reshape(rows, width).astype(jnp.bfloat16)
    row_v = grad_v_own.astype(jnp.bfloat16)
    h_t = h_one.T
    grad_wq = jnp.dot(h_t, row_q, preferred_element_type=jnp.float32).astype(jnp.bfloat16)
    grad_wk = jnp.dot(h_t, row_k, preferred_element_type=jnp.float32).astype(jnp.bfloat16)
    grad_wv = jnp.dot(h_t, row_v, preferred_element_type=jnp.float32).astype(jnp.bfloat16)
    grad_h_one = (
        jnp.dot(row_q, wq.T, preferred_element_type=jnp.float32)
        + jnp.dot(row_k, wk.T, preferred_element_type=jnp.float32)
        + jnp.dot(row_v, wv.T, preferred_element_type=jnp.float32)
    )
    grad_g_one = jnp.sum(grad_h_one * n_one, 0)
    grad_tokens = (grad_x_two + norm_back(grad_h_one * g_one, n_one, r_one)).astype(jnp.bfloat16)
    grad_gains = jnp.pad(jnp.stack([grad_g_one, grad_g_two], 1), ((0, 0), (0, 126)))
    sum_q = reduce_rows(jnp.concatenate([grad_wq, grad_gains.astype(jnp.bfloat16)], 1), 0)
    sum_k = reduce_rows(grad_wk, 1)
    sum_v = reduce_rows(grad_wv, 2)
    return (
        output[None],
        grad_tokens[None],
        jnp.concatenate([sum_q[:, :width], sum_k, sum_v], 1),
        sum_attn,
        jnp.concatenate([sum_ina, sum_ing], 1),
        sum_mlp.T,
        sum_q[:, width],
        sum_q[:, width + 1],
    )


def solution(mesh):
    in_specs = (
        P(("rep", "fsdp"), "cp", None),
        P(("rep", "fsdp"), "cp"),
        P(("rep", "fsdp"), "cp", None),
        P(("fsdp", "cp"), None),
        P(("fsdp", "cp"), None),
        P(("fsdp", "cp"), None),
        P(None, ("fsdp", "cp")),
        P(("fsdp", "cp")),
        P(("fsdp", "cp")),
    )
    out_specs = (
        P(("rep", "fsdp"), "cp", None),
        P(("rep", "fsdp"), "cp", None),
        P(("fsdp", "cp"), None),
        P(("fsdp", "cp"), None),
        P(("fsdp", "cp"), None),
        P(None, ("fsdp", "cp")),
        P(("fsdp", "cp")),
        P(("fsdp", "cp")),
    )
    return jax.shard_map(shards, mesh=mesh, in_specs=in_specs, out_specs=out_specs, check_vma=False)
```
